32 devices in a mesh: space: 2 (over y), chaos: 16 (over z, x, core).
Axes of the slice: x: 2, y: 2, z: 4, core: 2. Of those that a mesh axis runs over, the one named last changes fastest.
Arguments:
- kl_fields: float32 [9, 4, 16, 512], P(None, None, 'space'), may hold values from -5 to 5
- labels: int32 [4, 16, 512], P(None, 'space'), may hold values from 0 to 3
- region_scale: float32 [4, 9], replicated, may hold values from 0.5 to 2
- background: float32 [4, 16, 512], P(None, 'space'), may hold values from -4 to 4
- galerkin_table: int32 [384, 3], replicated, may hold values from 0 to 47, as said below
- triple_values: float32 [384], replicated, may hold values from -4 to 4
- direction: float32 [48, 3, 4, 16, 512], P('chaos', None, None, 'space'), may hold values from -6 to 6
Outputs:
- result: float32 [48, 3, 4, 16, 512], P('chaos', None, None, 'space')
The draws below stay inside these ranges and needn't reach their ends.
Inputs may be any that keep to these rules, and one draw needn't show every extreme that they name: `galerkin_table`: row r has term i = r // 8; the first row of each term is (i, i, 0); the others name any term j and a mode k of 1 to 8.
All inputs are finite; a program needn't handle non-finite values.
Results may differ from the reference program's by a relative error of at most 0.000076.
Values sent between devices are 32-bit elements; how exact they have to be, the bound alone decides.
A program may use at most 128 MiB of HBM per device.

```python
import math
import jax
import jax.numpy as jnp
from jax import lax

PLANES = 4
COLS = 512
MODES = 9
REGIONS = 4
PER_TERM = 8
CHAOS = 48
ROWS = 16
ENTRIES = 384


def draw_galerkin_table(key, part):
    total_rows = CHAOS * PER_TERM
    row_ids = jnp.arange(total_rows, dtype=jnp.int32)
    term_ids = row_ids // PER_TERM
    slot_ids = row_ids % PER_TERM
    source_ids = jax.random.randint(jax.random.fold_in(key, 11), (total_rows,), 0, CHAOS, dtype=jnp.int32)
    mode_ids = jax.random.randint(jax.random.fold_in(key, 23), (total_rows,), 1, MODES, dtype=jnp.int32)
    source_ids = jnp.where(slot_ids == 0, term_ids, source_ids)
    mode_ids = jnp.where(slot_ids == 0, 0, mode_ids)
    return jnp.stack([term_ids, source_ids, mode_ids], axis=1).astype(jnp.int32)


def with_ends(entries, key, smallest, largest):
    dims = entries.shape
    place = [jax.random.randint(jax.random.fold_in(key, axis), (), 0, dims[axis]) for axis in range(len(dims))]
    entries = entries.at[tuple(place)].set(smallest)
    longest = dims.index(max(dims))
    place[longest] = (place[longest] + 1) % dims[longest]
    return entries.at[tuple(place)].set(largest)


def block_scale(stream_key, shape, pieces, low, largest):
    factor_of, own = 1.0, jax.random.fold_in(stream_key, 6)
    for dim, blocks in pieces:
        heights = jnp.exp(jax.random.uniform(jax.random.fold_in(own, dim), (blocks,), jnp.float32, low / len(pieces), largest / len(pieces)))
        factor_of = factor_of * jnp.repeat(heights, shape[dim] // blocks).reshape([-1 if axis == dim else 1 for axis in range(len(shape))])
    return factor_of


def centred(own_key, shape, width, most, split=(), held_as=jnp.bfloat16):
    values = width * jax.random.normal(own_key, shape, jnp.float32)
    if split:
        values = values * block_scale(own_key, shape, split, -0.22, 0.18)
    return jnp.clip(values, -most, most).astype(held_as)


def setup_inputs(seed: int = 0) -> dict:
    arg_keys = jax.random.split(jax.random.key(seed), 8)
    return {
        "kl_fields": centred(arg_keys[0], (MODES, PLANES, ROWS, COLS), 1.0, 5.0, ((2, 2),), jnp.float32),
        "labels": with_ends(jax.random.randint(arg_keys[1], (PLANES, ROWS, COLS), 0, REGIONS), jax.random.fold_in(arg_keys[1], 1), 0, REGIONS - 1).astype(jnp.int32),
        "region_scale": jnp.clip(jnp.exp(jax.random.uniform(arg_keys[2], (REGIONS, MODES), jnp.float32, math.log(0.5), math.log(2.0))), 0.5, 2.0),
        "background": centred(arg_keys[3], (PLANES, ROWS, COLS), 1.0, 4.0, ((1, 2),), jnp.float32),
        "galerkin_table": draw_galerkin_table(jax.random.fold_in(arg_keys[7], 71), 0),
        "triple_values": centred(arg_keys[5], (ENTRIES,), 1.0, 4.0, (), jnp.float32),
        "direction": centred(arg_keys[6], (CHAOS, 3, PLANES, ROWS, COLS), 1.0, 6.0, ((0, 16), (3, 2)), jnp.float32),
    }


def neighbours(padded):
    middle = padded[..., 1:-1, :]
    row_next = padded[..., 2:, :]
    row_prev = padded[..., :-2, :]
    plane_zero = jnp.zeros_like(middle[..., :1, :, :])
    plane_next = jnp.concatenate([middle[..., 1:, :, :], plane_zero], axis=-3)
    plane_prev = jnp.concatenate([plane_zero, middle[..., :-1, :, :]], axis=-3)
    column_zero = jnp.zeros_like(middle[..., :1])
    column_next = jnp.concatenate([middle[..., 1:], column_zero], axis=-1)
    column_prev = jnp.concatenate([column_zero, middle[..., :-1]], axis=-1)
    return middle, (row_next, row_prev, plane_next, plane_prev, column_next, column_prev)


def drift_terms(potential_pad):
    middle, beside_all = neighbours(potential_pad)
    return tuple(0.5 * (other - middle) for other in beside_all)


def jacobian_block(coef_pad, potential_pad, electron_pad, hole_pad, drift_list):
    coef_mid, coef_nbr = neighbours(coef_pad)
    pot_mid, pot_nbr = neighbours(potential_pad)
    ele_mid, ele_nbr = neighbours(electron_pad)
    hole_mid, hole_nbr = neighbours(hole_pad)
    out_potential = coef_mid * (ele_mid - hole_mid)
    out_electron = jnp.zeros_like(out_potential)
    out_holes = jnp.zeros_like(out_potential)
    for facing in range(6):
        conduct = 0.5 * (coef_mid + coef_nbr[facing])
        potential_rise = pot_nbr[facing] - pot_mid
        drift_now = drift_list[facing]
        out_potential = out_potential - conduct * potential_rise
        out_electron = out_electron + conduct * ((ele_mid - ele_nbr[facing]) - drift_now * (ele_mid + ele_nbr[facing]) - potential_rise)
        out_holes = out_holes + conduct * ((hole_mid - hole_nbr[facing]) + drift_now * (hole_mid + hole_nbr[facing]) + potential_rise)
    return jnp.stack([out_potential, out_electron, out_holes], axis=-4)


def reference(kl_fields, labels, region_scale, background, galerkin_table, triple_values, direction):
    scaled = kl_fields * jnp.moveaxis(region_scale[labels], -1, 0)
    coef_pad = jnp.pad(scaled, ((0, 0), (0, 0), (1, 1), (0, 0)))
    drift_list = drift_terms(jnp.pad(background, ((0, 0), (1, 1), (0, 0))))
    field_pad = jnp.pad(direction, ((0, 0), (0, 0), (0, 0), (1, 1), (0, 0)))

    def visit(entry, carried):
        target = galerkin_table[entry, 0]
        source = galerkin_table[entry, 1]
        mode_index = galerkin_table[entry, 2]
        coef_now = lax.dynamic_index_in_dim(coef_pad, mode_index, 0, keepdims=False)
        fields = lax.dynamic_index_in_dim(field_pad, source, 0, keepdims=False)
        update = triple_values[entry] * jacobian_block(coef_now, fields[0], fields[1], fields[2], drift_list)
        current = lax.dynamic_index_in_dim(carried, target, 0, keepdims=False)
        return lax.dynamic_update_index_in_dim(carried, current + update, target, 0)

    return lax.fori_loop(0, galerkin_table.shape[0], visit, jnp.zeros(direction.shape, jnp.float32))
```

```python
import functools

import jax
import jax.numpy as jnp
from jax import lax
from jax.experimental import pallas as pl
from jax.experimental.pallas import tpu as pltpu
from jax.sharding import PartitionSpec as P

MESH = pl.DeviceIdType.MESH
FACES = 6


def offset_of(step, group):
    sign = 1 - 2 * (step % 2)
    return group // 2 + sign * ((step + 1) // 2)


def kernel(
    dims,
    kl,
    labels,
    background,
    direction,
    scale,
    table,
    values,
    out,
    send,
    recv,
    result,
    back,
    kl_tiles,
    label_tiles,
    coef,
    coef_halo,
    halo,
    conduct,
    drift,
    flux,
    send_sem,
    recv_sem,
    back_send_sem,
    back_recv_sem,
    row_send_sem,
    row_recv_sem,
):
    group, space, terms, fields, planes, width, modes, regions, per_term = dims
    count = terms * fields
    rows = direction.shape[2]
    lanes = planes * width
    blocks = lanes // width
    chunks = group // blocks
    me = lax.axis_index("chaos")
    here = lax.axis_index("space")

    lane = lax.broadcasted_iota(jnp.int32, (rows, lanes), 1)
    row = lax.broadcasted_iota(jnp.int32, (rows, lanes), 0)
    column = lane % width
    plane = lane // width

    barrier = pltpu.get_barrier_semaphore()
    for g in range(1, group):
        pl.semaphore_signal(
            barrier, inc=1, device_id={"chaos": lax.rem(me + g, group)}, device_id_type=MESH
        )

    @pl.when(here > 0)
    def _():
        pl.semaphore_signal(barrier, inc=1, device_id={"space": here - 1}, device_id_type=MESH)

    @pl.when(here < space - 1)
    def _():
        pl.semaphore_signal(barrier, inc=1, device_id={"space": here + 1}, device_id_type=MESH)

    def turn(tile, shift, axis=1):
        shift = shift % tile.shape[axis]
        return tile if shift == 0 else pltpu.roll(tile, shift, axis)

    def swap_blocks(tiles):
        swapped = []
        for m in range(blocks):
            tile = tiles[0] if m == 0 else turn(tiles[0], -width * m)
            for p in range(1, blocks):
                tile = jnp.where(plane == p, turn(tiles[p], width * (p - m)), tile)
            swapped.append(tile)
        return swapped

    @pl.loop(0, count)
    def _(n):
        for q in range(chunks):
            part = [direction[n, p, :, lanes * q : lanes * (q + 1)] for p in range(planes)]
            for m, tile in enumerate(swap_blocks(part)):
                send[blocks * q + m, n] = tile

    half = width // 2

    @pl.loop(0, group)
    def _(d):
        after = jnp.minimum(d + 1, group - 1)
        before = jnp.maximum(d - 1, 0)
        right = jnp.zeros((rows, lanes), jnp.float32)
        left = jnp.zeros((rows, lanes), jnp.float32)
        for n in range(count):
            right = jnp.where(column == n, turn(send[after, n], n), right)
            left = jnp.where(column == half + n, turn(send[before, n], half + n - (width - 1)), left)
        right = jnp.where(d < group - 1, right, 0.0)
        left = jnp.where(d > 0, left, 0.0)
        send[d, count] = jnp.where(column < half, right, left)

    beside = jnp.minimum(here, 1) + jnp.minimum(space - 1 - here, 1)
    pl.semaphore_wait(barrier, group - 1 + beside)

    def forth(source, target):
        return pltpu.make_async_remote_copy(
            src_ref=send.at[target],
            dst_ref=recv.at[source],
            send_sem=send_sem.at[target],
            recv_sem=recv_sem.at[source],
            device_id={"chaos": target},
            device_id_type=MESH,
        )

    @pl.loop(0, group - 1)
    def _(step):
        forth(me, lax.rem(me + offset_of(step, group), group)).start()

    @pl.loop(0, count + 1)
    def _(n):
        recv[me, n] = send[me, n]

    @pl.loop(0, modes)
    def _(k):
        for q in range(chunks):
            part = [kl[k, p, :, lanes * q : lanes * (q + 1)] for p in range(planes)]
            for m, tile in enumerate(swap_blocks(part)):
                kl_tiles[blocks * q + m, k] = tile

    for q in range(chunks):
        part = [background[p, :, lanes * q : lanes * (q + 1)] for p in range(planes)]
        for m, tile in enumerate(swap_blocks(part)):
            kl_tiles[blocks * q + m, modes] = tile
        part = [labels[p, :, lanes * q : lanes * (q + 1)] for p in range(planes)]
        for m, tile in enumerate(swap_blocks(part)):
            label_tiles[blocks * q + m] = tile

    places = (me, jnp.minimum(me + 1, group - 1), jnp.maximum(me - 1, 0))
    inside = (None, me < group - 1, me > 0)
    for slot, (place, ok) in enumerate(zip(places, inside)):
        region_tile = label_tiles[place]
        for k in range(modes):
            lookup = jnp.full((rows, lanes), scale[0, k])
            for region in range(1, regions):
                lookup = jnp.where(region_tile == region, scale[region, k], lookup)
            tile = kl_tiles[place, k] * lookup
            coef[slot, k] = tile if ok is None else jnp.where(ok, tile, 0.0)
        tile = kl_tiles[place, modes]
        coef[slot, modes] = tile if ok is None else jnp.where(ok, tile, 0.0)


    def row_copy(part, way):
        buffer = (coef_halo, halo)[part]
        return pltpu.make_async_remote_copy(
            src_ref=buffer.at[way],
            dst_ref=buffer.at[2 + way],
            send_sem=row_send_sem.at[part, way],
            recv_sem=row_recv_sem.at[part, way],
            device_id={"space": here + (1 if way == 0 else -1)},
            device_id_type=MESH,
        )

    def start_rows(part):
        @pl.when(here < space - 1)
        def _():
            row_copy(part, 0).start()

        @pl.when(here > 0)
        def _():
            row_copy(part, 1).start()

    def finish_rows(part):
        buffer = (coef_halo, halo)[part]

        @pl.when(here > 0)
        def _():
            row_copy(part, 0).wait_recv()

        @pl.when(here < space - 1)
        def _():
            row_copy(part, 1).wait_recv()

        @pl.when(here == 0)
        def _():
            buffer[2] = jnp.zeros(buffer.shape[1:], jnp.float32)

        @pl.when(here == space - 1)
        def _():
            buffer[3] = jnp.zeros(buffer.shape[1:], jnp.float32)

        @pl.when(here < space - 1)
        def _():
            row_copy(part, 0).wait_send()

        @pl.when(here > 0)
        def _():
            row_copy(part, 1).wait_send()

    for k in range(modes + 1):
        coef_halo[0, k] = coef[0, k, rows - 1 : rows, :]
        coef_halo[1, k] = coef[0, k, 0:1, :]

    def side_neighbours(tile, after, before):
        return (
            jnp.where(plane < planes - 1, turn(tile, -width), 0.0),
            jnp.where(plane > 0, turn(tile, width), 0.0),
            jnp.where(column == width - 1, after, turn(tile, -1)),
            jnp.where(column == 0, before, turn(tile, 1)),
        )

    def row_neighbours(tile, above, below):
        return (
            jnp.where(row == rows - 1, jnp.broadcast_to(below, tile.shape), turn(tile, -1, 0)),
            jnp.where(row == 0, jnp.broadcast_to(above, tile.shape), turn(tile, 1, 0)),
        )

    start_rows(0)

    for k in range(modes + 1):
        tile = coef[0, k]
        others = side_neighbours(
            tile, turn(coef[1, k], width - 1), turn(coef[2, k], 1 - width)
        )
        for face, other in enumerate(others):
            if k < modes:
                conduct[k, 2 + face] = 0.5 * (tile + other)
            else:
                drift[2 + face] = 0.5 * (other - tile)
        if k < modes:
            conduct[k, FACES] = tile

    finish_rows(0)
    for k in range(modes + 1):
        tile = coef[0, k]
        for face, other in enumerate(row_neighbours(tile, coef_halo[2, k], coef_halo[3, k])):
            if k < modes:
                conduct[k, face] = 0.5 * (tile + other)
            else:
                drift[face] = 0.5 * (other - tile)

    def store_flux(j, face, tiles, others):
        slope = drift[face]
        (u, v, w), (un, vn, wn) = tiles, others
        rise = un - u
        flux[j, 3 * face] = -rise
        flux[j, 3 * face + 1] = (v - vn) - slope * (v + vn) - rise
        flux[j, 3 * face + 2] = (w - wn) + slope * (w + wn) + rise

    @pl.loop(0, group)
    def _(step):
        source = lax.rem(me + group - offset_of(group - 1 - step, group), group)

        @pl.when(step > 0)
        def _():
            forth(source, source).wait_recv()

        rim = recv[source, count]
        for t in range(terms):
            j = source * terms + t
            tiles = [recv[source, t * fields + f] for f in range(fields)]
            others = []
            for f in range(fields):
                n = t * fields + f
                halo[0, source * count + n] = tiles[f][rows - 1 : rows]
                halo[1, source * count + n] = tiles[f][0:1]
                others.append(
                    side_neighbours(
                        tiles[f], turn(rim, width - 1 - n), turn(rim, -half - n)
                    )
                )
            for face in range(4):
                store_flux(j, 2 + face, tiles, [o[face] for o in others])
            flux[j, 3 * FACES] = tiles[1] - tiles[2]

    start_rows(1)
    finish_rows(1)

    @pl.loop(0, group)
    def _(source):
        for t in range(terms):
            j = source * terms + t
            tiles = [recv[source, t * fields + f] for f in range(fields)]
            others = [
                row_neighbours(
                    tiles[f],
                    halo[2, source * count + t * fields + f],
                    halo[3, source * count + t * fields + f],
                )
                for f in range(fields)
            ]
            for face in range(2):
                store_flux(j, face, tiles, [o[face] for o in others])

    def home(source, target):
        return pltpu.make_async_remote_copy(
            src_ref=result.at[target],
            dst_ref=back.at[source],
            send_sem=back_send_sem.at[target],
            recv_sem=back_recv_sem.at[source],
            device_id={"chaos": target},
            device_id_type=MESH,
        )

    @pl.loop(0, group)
    def _(step):
        target = lax.rem(me + offset_of(step, group), group)
        for t in range(terms):
            total = [jnp.zeros((rows, lanes), jnp.float32) for _ in range(fields)]
            for e in range(per_term):
                entry = (target * terms + t) * per_term + e
                j, k, value = table[0, entry], table[1, entry], values[entry]
                total[0] += (value * conduct[k, FACES]) * flux[j, 3 * FACES]
                for face in range(FACES):
                    h = value * conduct[k, face]
                    for f in range(fields):
                        total[f] += h * flux[j, 3 * face + f]
            for f in range(fields):
                result[target, t * fields + f] = total[f]

        @pl.when(step > 0)
        def _():
            home(me, lax.rem(me + offset_of(step - 1, group), group)).start()

    @pl.loop(0, count)
    def _(n):
        back[me, n] = result[me, n]

    @pl.loop(0, group - 1)
    def _(step):
        other = lax.rem(me + offset_of(group - 2 - step, group), group)
        home(other, other).wait_recv()

    @pl.loop(0, count)
    def _(n):
        for q in range(chunks):
            part = [back[blocks * q + m, n] for m in range(blocks)]
            for p, tile in enumerate(swap_blocks(part)):
                out[n, p, :, lanes * q : lanes * (q + 1)] = tile

    @pl.loop(0, group - 1)
    def _(step):
        target = lax.rem(me + offset_of(step, group), group)
        forth(me, target).wait_send()
        home(me, target).wait_send()


def solution(mesh):
    group, space = mesh.shape["chaos"], mesh.shape["space"]

    def shards(kl_fields, labels, region_scale, background, galerkin_table, triple_values, direction):
        terms, fields, planes, rows, columns = direction.shape
        modes, regions = kl_fields.shape[0], region_scale.shape[0]
        width = columns // group
        lanes = planes * width
        count = terms * fields
        all_terms = terms * group
        per_term = galerkin_table.shape[0] // all_terms
        dims = (group, space, terms, fields, planes, width, modes, regions, per_term)
        table = galerkin_table[:, 1:].T
        vmem = pl.BlockSpec(memory_space=pltpu.VMEM)
        smem = pl.BlockSpec(memory_space=pltpu.SMEM)
        f32 = jnp.float32
        out = pl.pallas_call(
            functools.partial(kernel, dims),
            out_shape=jax.ShapeDtypeStruct((count, planes, rows, columns), f32),
            in_specs=[vmem] * 4 + [smem] * 3,
            out_specs=vmem,
            scratch_shapes=[
                pltpu.VMEM((group, count + 1, rows, lanes), f32),
                pltpu.VMEM((group, count + 1, rows, lanes), f32),
                pltpu.VMEM((group, count, rows, lanes), f32),
                pltpu.VMEM((group, count, rows, lanes), f32),
                pltpu.VMEM((group, modes + 1, rows, lanes), f32),
                pltpu.VMEM((group, rows, lanes), jnp.int32),
                pltpu.VMEM((3, modes + 1, rows, lanes), f32),
                pltpu.VMEM((4, modes + 1, 1, lanes), f32),
                pltpu.VMEM((4, group * count, 1, lanes), f32),
                pltpu.VMEM((modes, FACES + 1, rows, lanes), f32),
                pltpu.VMEM((FACES, rows, lanes), f32),
                pltpu.VMEM((all_terms, 3 * FACES + 1, rows, lanes), f32),
                pltpu.SemaphoreType.DMA((group,)),
                pltpu.SemaphoreType.DMA((group,)),
                pltpu.SemaphoreType.DMA((group,)),
                pltpu.SemaphoreType.DMA((group,)),
                pltpu.SemaphoreType.DMA((2, 2)),
                pltpu.SemaphoreType.DMA((2, 2)),
            ],
            compiler_params=pltpu.CompilerParams(
                collective_id=0, has_side_effects=True, vmem_limit_bytes=40 << 20
            ),
        )(
            kl_fields,
            labels,
            background,
            direction.reshape(count, planes, rows, columns),
            region_scale,
            table,
            triple_values,
        )
        return out.reshape(direction.shape)

    return jax.shard_map(
        shards,
        mesh=mesh,
        in_specs=(
            P(None, None, "space", None),
            P(None, "space", None),
            P(),
            P(None, "space", None),
            P(),
            P(),
            P("chaos", None, None, "space", None),
        ),
        out_specs=P("chaos", None, None, "space", None),
        check_vma=False,
    )
```

```python
import functools
import math

import jax
import jax.numpy as jnp
from jax import lax
from jax.experimental import pallas as pl
from jax.experimental.pallas import tpu as pltpu
from jax.sharding import PartitionSpec as P

MESH = pl.DeviceIdType.MESH
FACES = 6
VMEM_BYTES = 67043328


def peer_of(me, step, group):
    half = group // 2
    mine = half * (me // half)
    cross = half - mine + (me + step) % half
    near = mine + (me + step + 1) % half
    return jnp.where(step < half, cross, near)


def kernel(
    dims,
    kl_hbm,
    labels_hbm,
    background_hbm,
    direction_hbm,
    scale_hbm,
    table_hbm,
    values_hbm,
    out,
    kl,
    labels,
    background,
    direction,
    scale,
    table,
    values,
    send,
    recv,
    result,
    back,
    kl_tiles,
    label_tiles,
    coef,
    coef_halo,
    row_halo,
    column_halo,
    conduct,
    drift,
    flux,
    centre,
    load_sem,
    send_sem,
    recv_sem,
    back_send_sem,
    back_recv_sem,
    row_send_sem,
    row_recv_sem,
    column_send_sem,
    column_recv_sem,
):
    group, space, terms, fields, planes, width, modes, regions, per_term, packed = dims
    rows = direction.shape[2]
    lanes = planes * width
    blocks = lanes // width
    chunks = group // blocks
    all_terms = group * terms
    me = lax.axis_index("chaos")
    here = lax.axis_index("space")

    loads = [
        pltpu.make_async_copy(source, target, load_sem.at[n])
        for n, (source, target) in enumerate(
            (
                (direction_hbm, direction),
                (kl_hbm, kl),
                (labels_hbm, labels),
                (background_hbm, background),
                (scale_hbm, scale),
                (table_hbm, table),
                (values_hbm, values),
            )
        )
    ]
    for load in loads:
        load.start()

    barrier = pltpu.get_barrier_semaphore()
    for g in range(1, group):
        pl.semaphore_signal(
            barrier, inc=1, device_id={"chaos": lax.rem(me + g, group)}, device_id_type=MESH
        )

    @pl.when(here > 0)
    def _():
        pl.semaphore_signal(barrier, inc=1, device_id={"space": here - 1}, device_id_type=MESH)

    @pl.when(here < space - 1)
    def _():
        pl.semaphore_signal(barrier, inc=1, device_id={"space": here + 1}, device_id_type=MESH)

    lane = lax.broadcasted_iota(jnp.int32, (rows, lanes), 1)
    row = lax.broadcasted_iota(jnp.int32, (rows, lanes), 0)
    column = lane % width
    plane = lane // width

    def turn(tile, shift, axis=1):
        shift = shift % tile.shape[axis]
        return tile if shift == 0 else pltpu.roll(tile, shift, axis)

    def swap_blocks(tiles):
        swapped = []
        for m in range(blocks):
            tile = tiles[0] if m == 0 else turn(tiles[0], -width * m)
            for p in range(1, blocks):
                tile = jnp.where(plane == p, turn(tiles[p], width * (p - m)), tile)
            swapped.append(tile)
        return swapped

    loads[0].wait()

    @pl.loop(0, fields)
    def _(f):
        for t in range(terms):
            for q in range(chunks):
                part = [
                    direction[t * fields + f, p, :, lanes * q : lanes * (q + 1)]
                    for p in range(planes)
                ]
                for m, tile in enumerate(swap_blocks(part)):
                    send[f, blocks * q + m, t] = tile

    beside = jnp.minimum(here, 1) + jnp.minimum(space - 1 - here, 1)
    pl.semaphore_wait(barrier, group - 1 + beside)

    def forth(f, source, target):
        return pltpu.make_async_remote_copy(
            src_ref=send.at[f, target],
            dst_ref=recv.at[f, source],
            send_sem=send_sem.at[f, target],
            recv_sem=recv_sem.at[f, source],
            device_id={"chaos": target},
            device_id_type=MESH,
        )

    for f in range(fields):

        @pl.loop(0, group - 1)
        def _(step):
            forth(f, me, peer_of(me, step, group)).start()

        for t in range(terms):
            recv[f, me, t] = send[f, me, t]

    for load in loads[1:]:
        load.wait()

    @pl.loop(0, modes)
    def _(k):
        for q in range(chunks):
            part = [kl[k, p, :, lanes * q : lanes * (q + 1)] for p in range(planes)]
            for m, tile in enumerate(swap_blocks(part)):
                kl_tiles[blocks * q + m, k] = tile

    for q in range(chunks):
        part = [background[p, :, lanes * q : lanes * (q + 1)] for p in range(planes)]
        for m, tile in enumerate(swap_blocks(part)):
            kl_tiles[blocks * q + m, modes] = tile
        part = [labels[p, :, lanes * q : lanes * (q + 1)] for p in range(planes)]
        for m, tile in enumerate(swap_blocks(part)):
            label_tiles[blocks * q + m] = tile

    places = (me, jnp.minimum(me + 1, group - 1), jnp.maximum(me - 1, 0))
    inside = (None, me < group - 1, me > 0)
    for slot, (place, ok) in enumerate(zip(places, inside)):
        region_tile = label_tiles[place]
        for k in range(modes):
            lookup = jnp.full((rows, lanes), scale[0, k])
            for region in range(1, regions):
                lookup = jnp.where(region_tile == region, scale[region, k], lookup)
            tile = kl_tiles[place, k] * lookup
            coef[slot, k] = tile if ok is None else jnp.where(ok, tile, 0.0)
        tile = kl_tiles[place, modes]
        coef[slot, modes] = tile if ok is None else jnp.where(ok, tile, 0.0)

    def exchange(buffer, axis, position, size, send_sems, recv_sems):
        def copy(way):
            return pltpu.make_async_remote_copy(
                src_ref=buffer.at[way],
                dst_ref=buffer.at[2 + way],
                send_sem=send_sems.at[way],
                recv_sem=recv_sems.at[way],
                device_id={axis: position + 1 - 2 * way},
                device_id_type=MESH,
            )

        def start():
            @pl.when(position < size - 1)
            def _():
                copy(0).start()

            @pl.when(position > 0)
            def _():
                copy(1).start()

        def finish():
            @pl.when(position > 0)
            def _():
                copy(0).wait_recv()

            @pl.when(position < size - 1)
            def _():
                copy(1).wait_recv()

            @pl.when(position == 0)
            def _():
                buffer[2] = jnp.zeros(buffer.shape[1:], jnp.float32)

            @pl.when(position == size - 1)
            def _():
                buffer[3] = jnp.zeros(buffer.shape[1:], jnp.float32)

            @pl.when(position < size - 1)
            def _():
                copy(0).wait_send()

            @pl.when(position > 0)
            def _():
                copy(1).wait_send()

        return start, finish

    def side_neighbours(tile, before, after):
        return (
            jnp.where(plane < planes - 1, turn(tile, -width), 0.0),
            jnp.where(plane > 0, turn(tile, width), 0.0),
            jnp.where(column == width - 1, after, turn(tile, -1)),
            jnp.where(column == 0, before, turn(tile, 1)),
        )

    def row_neighbours(tile, above, below):
        return (
            jnp.where(row == rows - 1, jnp.broadcast_to(below, tile.shape), turn(tile, -1, 0)),
            jnp.where(row == 0, jnp.broadcast_to(above, tile.shape), turn(tile, 1, 0)),
        )

    for k in range(modes + 1):
        coef_halo[0, k] = coef[0, k, rows - 1 : rows, :]
        coef_halo[1, k] = coef[0, k, 0:1, :]

    start_coef, finish_coef = exchange(
        coef_halo, "space", here, space, row_send_sem.at[fields], row_recv_sem.at[fields]
    )
    start_coef()
    finish_coef()
    for k in range(modes + 1):
        tile = coef[0, k]
        others = row_neighbours(tile, coef_halo[2, k], coef_halo[3, k]) + side_neighbours(
            tile, turn(coef[2, k], 1 - width), turn(coef[1, k], width - 1)
        )
        for face, other in enumerate(others):
            if k < modes:
                conduct[k, face] = 0.5 * (tile + other)
            else:
                drift[face] = 0.5 * (other - tile)
        if k < modes:
            conduct[k, FACES] = tile

    def home(f, source, target):
        return pltpu.make_async_remote_copy(
            src_ref=result.at[f, target],
            dst_ref=back.at[f, source],
            send_sem=back_send_sem.at[f, target],
            recv_sem=back_recv_sem.at[f, source],
            device_id={"chaos": target},
            device_id_type=MESH,
        )

    def gather_field(f):
        @pl.loop(0, group)
        def _(step):
            source = peer_of(me, step, group)

            @pl.when(step < group - 1)
            def _():
                forth(f, source, source).wait_recv()

            for t in range(terms):
                tile = recv[f, source, t]
                row_halo[f, 0, source * terms + t] = tile[rows - 1 : rows]
                row_halo[f, 1, source * terms + t] = tile[0:1]

        start_rows, finish_rows = exchange(
            row_halo.at[f], "space", here, space, row_send_sem.at[f], row_recv_sem.at[f]
        )
        start_rows()

        @pl.loop(0, all_terms // packed)
        def _(g):
            last = jnp.zeros((rows, lanes), jnp.float32)
            first = jnp.zeros((rows, lanes), jnp.float32)
            for n in range(packed):
                j = g * packed + n
                tile = recv[f, j // terms, j % terms]
                last = jnp.where(column == n, turn(tile, n - (width - 1)), last)
                first = jnp.where(column == n, turn(tile, n), first)
            column_halo[f, 0, g] = last
            column_halo[f, 1, g] = first

        start_columns, finish_columns = exchange(
            column_halo.at[f], "chaos", me, group, column_send_sem.at[f], column_recv_sem.at[f]
        )
        start_columns()
        finish_rows()
        finish_columns()

    def flux_of(f):
        @pl.loop(0, all_terms // packed)
        def _(g):
            before, after = column_halo[f, 2, g], column_halo[f, 3, g]
            for n in range(packed):
                j = g * packed + n
                tile = recv[f, j // terms, j % terms]
                others = row_neighbours(
                    tile, row_halo[f, 2, j], row_halo[f, 3, j]
                ) + side_neighbours(tile, turn(before, -n), turn(after, width - 1 - n))
                for face, other in enumerate(others):
                    if f == 0:
                        flux[0, j, face] = tile - other
                    elif f == 1:
                        flux[1, j, face] = (
                            (tile - other) - drift[face] * (tile + other) + flux[0, j, face]
                        )
                    else:
                        flux[2, j, face] = (
                            (tile - other) + drift[face] * (tile + other) - flux[0, j, face]
                        )
                if f == 2:
                    centre[j] = recv[1, j // terms, j % terms] - tile

    def apply(which):
        def send_home(step):
            for f in which:
                home(f, me, peer_of(me, step, group)).start()

        @pl.loop(0, group)
        def _(step):
            target = peer_of(me, step, group)
            for t in range(terms):
                total = {f: jnp.zeros((rows, lanes), jnp.float32) for f in which}
                for e in range(per_term):
                    entry = (target * terms + t) * per_term + e
                    j, k, value = table[1, entry], table[2, entry], values[entry]
                    if 0 in which:
                        total[0] += (value * conduct[k, FACES]) * centre[j]
                    for face in range(FACES):
                        h = value * conduct[k, face]
                        for f in which:
                            total[f] += h * flux[f, j, face]
                for f in which:
                    result[f, target, t] = total[f]

            @pl.when(step > 0)
            def _():
                send_home(step - 1)

        for f in which:
            for t in range(terms):
                back[f, me, t] = result[f, me, t]

    def place_field(f):
        @pl.loop(0, group - 1)
        def _(step):
            other = peer_of(me, step, group)
            home(f, other, other).wait_recv()

        @pl.loop(0, terms)
        def _(t):
            for q in range(chunks):
                part = [back[f, blocks * q + m, t] for m in range(blocks)]
                for p, tile in enumerate(swap_blocks(part)):
                    out[t * fields + f, p, :, lanes * q : lanes * (q + 1)] = tile

    gather_field(0)
    flux_of(0)
    gather_field(1)
    flux_of(1)
    apply((1,))
    gather_field(2)
    flux_of(2)
    apply((0, 2))
    for f in (1, 0, 2):
        place_field(f)

    @pl.loop(0, group - 1)
    def _(step):
        target = peer_of(me, step, group)
        for f in range(fields):
            forth(f, me, target).wait_send()
            home(f, me, target).wait_send()


def solution(mesh):
    group, space = mesh.shape["chaos"], mesh.shape["space"]

    def shards(kl_fields, labels, region_scale, background, galerkin_table, triple_values, direction):
        terms, fields, planes, rows, columns = direction.shape
        modes, regions = kl_fields.shape[0], region_scale.shape[0]
        width = columns // group
        lanes = planes * width
        count = terms * fields
        all_terms = terms * group
        per_term = galerkin_table.shape[0] // all_terms
        packed = math.gcd(all_terms, width)
        dims = (group, space, terms, fields, planes, width, modes, regions, per_term, packed)
        table = galerkin_table.T
        hbm = pl.BlockSpec(memory_space=pltpu.HBM)
        f32 = jnp.float32
        tile = (rows, lanes)
        dma = pltpu.SemaphoreType.DMA
        out = pl.pallas_call(
            functools.partial(kernel, dims),
            out_shape=jax.ShapeDtypeStruct((count, planes, rows, columns), f32),
            in_specs=[hbm] * 7,
            out_specs=pl.BlockSpec(memory_space=pltpu.VMEM),
            scratch_shapes=[
                pltpu.VMEM(kl_fields.shape, f32),
                pltpu.VMEM(labels.shape, jnp.int32),
                pltpu.VMEM(background.shape, f32),
                pltpu.VMEM((count, planes, rows, columns), f32),
                pltpu.SMEM(region_scale.shape, f32),
                pltpu.SMEM(table.shape, jnp.int32),
                pltpu.SMEM(triple_values.shape, f32),
                pltpu.VMEM((fields, group, terms) + tile, f32),
                pltpu.VMEM((fields, group, terms) + tile, f32),
                pltpu.VMEM((fields, group, terms) + tile, f32),
                pltpu.VMEM((fields, group, terms) + tile, f32),
                pltpu.VMEM((group, modes + 1) + tile, f32),
                pltpu.VMEM((group,) + tile, jnp.int32),
                pltpu.VMEM((3, modes + 1) + tile, f32),
                pltpu.VMEM((4, modes + 1, 1, lanes), f32),
                pltpu.VMEM((fields, 4, all_terms, 1, lanes), f32),
                pltpu.VMEM((fields, 4, all_terms // packed) + tile, f32),
                pltpu.VMEM((modes, FACES + 1) + tile, f32),
                pltpu.VMEM((FACES,) + tile, f32),
                pltpu.VMEM((fields, all_terms, FACES) + tile, f32),
                pltpu.VMEM((all_terms,) + tile, f32),
                dma((7,)),
                dma((fields, group)),
                dma((fields, group)),
                dma((fields, group)),
                dma((fields, group)),
                dma((fields + 1, 2)),
                dma((fields + 1, 2)),
                dma((fields, 2)),
                dma((fields, 2)),
            ],
            compiler_params=pltpu.CompilerParams(
                collective_id=0, has_side_effects=True, vmem_limit_bytes=VMEM_BYTES
            ),
        )(
            kl_fields,
            labels,
            background,
            direction.reshape(count, planes, rows, columns),
            region_scale,
            table,
            triple_values,
        )
        return out.reshape(direction.shape)

    return jax.shard_map(
        shards,
        mesh=mesh,
        in_specs=(
            P(None, None, "space", None),
            P(None, "space", None),
            P(),
            P(None, "space", None),
            P(),
            P(),
            P("chaos", None, None, "space", None),
        ),
        out_specs=P("chaos", None, None, "space", None),
        check_vma=False,
    )
```

```python
import functools

import jax
import jax.numpy as jnp
from jax import lax
from jax.experimental import pallas as pl
from jax.experimental.pallas import tpu as pltpu
from jax.sharding import PartitionSpec as P

MESH = pl.DeviceIdType.MESH
FACES = 6
VMEM_BYTES = 40 << 20


def peer_of(me, step, group):
    half = group // 2
    mine = half * (me // half)
    cross = half - mine + (me + step) % half
    near = mine + (me + step + 1) % half
    return jnp.where(step < half, cross, near)


def kernel(
    dims,
    kl_hbm,
    labels_hbm,
    background_hbm,
    direction_hbm,
    scale_hbm,
    table_hbm,
    values_hbm,
    out,
    kl,
    labels,
    background,
    direction,
    scale,
    table,
    values,
    send,
    recv,
    result,
    back,
    kl_tiles,
    label_tiles,
    coef,
    coef_halo,
    row_halo,
    conduct,
    drift,
    flux,
    centre,
    load_sem,
    send_sem,
    recv_sem,
    back_send_sem,
    back_recv_sem,
    row_send_sem,
    row_recv_sem,
):
    group, space, terms, fields, planes, width, modes, regions, per_term = dims
    rows = direction.shape[2]
    lanes = planes * width
    blocks = lanes // width
    chunks = group // blocks
    me = lax.axis_index("chaos")
    here = lax.axis_index("space")

    loads = [
        pltpu.make_async_copy(source, target, load_sem.at[n])
        for n, (source, target) in enumerate(
            (
                (direction_hbm, direction),
                (kl_hbm, kl),
                (labels_hbm, labels),
                (background_hbm, background),
                (scale_hbm, scale),
                (table_hbm, table),
                (values_hbm, values),
            )
        )
    ]
    for load in loads:
        load.start()

    barrier = pltpu.get_barrier_semaphore()
    for g in range(1, group):
        pl.semaphore_signal(
            barrier, inc=1, device_id={"chaos": lax.rem(me + g, group)}, device_id_type=MESH
        )

    @pl.when(here > 0)
    def _():
        pl.semaphore_signal(barrier, inc=1, device_id={"space": here - 1}, device_id_type=MESH)

    @pl.when(here < space - 1)
    def _():
        pl.semaphore_signal(barrier, inc=1, device_id={"space": here + 1}, device_id_type=MESH)

    lane = lax.broadcasted_iota(jnp.int32, (rows, lanes), 1)
    row = lax.broadcasted_iota(jnp.int32, (rows, lanes), 0)
    column = lane % width
    plane = lane // width

    def turn(tile, shift, axis=1):
        shift = shift % tile.shape[axis]
        return tile if shift == 0 else pltpu.roll(tile, shift, axis)

    def swap_blocks(tiles):
        swapped = []
        for m in range(blocks):
            tile = tiles[0] if m == 0 else turn(tiles[0], -width * m)
            for p in range(1, blocks):
                tile = jnp.where(plane == p, turn(tiles[p], width * (p - m)), tile)
            swapped.append(tile)
        return swapped

    loads[0].wait()

    @pl.loop(0, fields)
    def _(f):
        for t in range(terms):
            for q in range(chunks):
                part = [
                    direction[t * fields + f, p, :, lanes * q : lanes * (q + 1)]
                    for p in range(planes)
                ]
                for m, tile in enumerate(swap_blocks(part)):
                    send[f, blocks * q + m, t] = tile

    half = width // 2

    @pl.loop(0, group)
    def _(d):
        after = jnp.minimum(d + 1, group - 1)
        before = jnp.maximum(d - 1, 0)
        right = jnp.zeros((rows, lanes), jnp.float32)
        left = jnp.zeros((rows, lanes), jnp.float32)
        for f in range(fields):
            for t in range(terms):
                n = f * terms + t
                right = jnp.where(column == n, turn(send[f, after, t], n), right)
                left = jnp.where(
                    column == half + n, turn(send[f, before, t], half + n - (width - 1)), left
                )
        right = jnp.where(d < group - 1, right, 0.0)
        left = jnp.where(d > 0, left, 0.0)
        send[0, d, terms] = jnp.where(column < half, right, left)

    beside = jnp.minimum(here, 1) + jnp.minimum(space - 1 - here, 1)
    pl.semaphore_wait(barrier, group - 1 + beside)

    def forth(f, source, target):
        size = terms + 1 if f == 0 else terms
        return pltpu.make_async_remote_copy(
            src_ref=send.at[f, target, pl.ds(0, size)],
            dst_ref=recv.at[f, source, pl.ds(0, size)],
            send_sem=send_sem.at[f, target],
            recv_sem=recv_sem.at[f, source],
            device_id={"chaos": target},
            device_id_type=MESH,
        )

    for f in range(fields):

        @pl.loop(0, group - 1)
        def _(step):
            forth(f, me, peer_of(me, step, group)).start()

        for t in range(terms + 1 if f == 0 else terms):
            recv[f, me, t] = send[f, me, t]

    for load in loads[1:]:
        load.wait()

    @pl.loop(0, modes)
    def _(k):
        for q in range(chunks):
            part = [kl[k, p, :, lanes * q : lanes * (q + 1)] for p in range(planes)]
            for m, tile in enumerate(swap_blocks(part)):
                kl_tiles[blocks * q + m, k] = tile

    for q in range(chunks):
        part = [background[p, :, lanes * q : lanes * (q + 1)] for p in range(planes)]
        for m, tile in enumerate(swap_blocks(part)):
            kl_tiles[blocks * q + m, modes] = tile
        part = [labels[p, :, lanes * q : lanes * (q + 1)] for p in range(planes)]
        for m, tile in enumerate(swap_blocks(part)):
            label_tiles[blocks * q + m] = tile

    places = (me, jnp.minimum(me + 1, group - 1), jnp.maximum(me - 1, 0))
    inside = (None, me < group - 1, me > 0)
    for slot, (place, ok) in enumerate(zip(places, inside)):
        region_tile = label_tiles[place]
        for k in range(modes):
            lookup = jnp.full((rows, lanes), scale[0, k])
            for region in range(1, regions):
                lookup = jnp.where(region_tile == region, scale[region, k], lookup)
            tile = kl_tiles[place, k] * lookup
            coef[slot, k] = tile if ok is None else jnp.where(ok, tile, 0.0)
        tile = kl_tiles[place, modes]
        coef[slot, modes] = tile if ok is None else jnp.where(ok, tile, 0.0)

    def exchange(buffer, axis, position, size, send_sems, recv_sems):
        def copy(way):
            return pltpu.make_async_remote_copy(
                src_ref=buffer.at[way],
                dst_ref=buffer.at[2 + way],
                send_sem=send_sems.at[way],
                recv_sem=recv_sems.at[way],
                device_id={axis: position + 1 - 2 * way},
                device_id_type=MESH,
            )

        def start():
            @pl.when(position < size - 1)
            def _():
                copy(0).start()

            @pl.when(position > 0)
            def _():
                copy(1).start()

        def finish():
            @pl.when(position > 0)
            def _():
                copy(0).wait_recv()

            @pl.when(position < size - 1)
            def _():
                copy(1).wait_recv()

            @pl.when(position == 0)
            def _():
                buffer[2] = jnp.zeros(buffer.shape[1:], jnp.float32)

            @pl.when(position == size - 1)
            def _():
                buffer[3] = jnp.zeros(buffer.shape[1:], jnp.float32)

            @pl.when(position < size - 1)
            def _():
                copy(0).wait_send()

            @pl.when(position > 0)
            def _():
                copy(1).wait_send()

        return start, finish

    def side_neighbours(tile, before, after):
        return (
            jnp.where(plane < planes - 1, turn(tile, -width), 0.0),
            jnp.where(plane > 0, turn(tile, width), 0.0),
            jnp.where(column == width - 1, after, turn(tile, -1)),
            jnp.where(column == 0, before, turn(tile, 1)),
        )

    def row_neighbours(tile, above, below):
        return (
            jnp.where(row == rows - 1, jnp.broadcast_to(below, tile.shape), turn(tile, -1, 0)),
            jnp.where(row == 0, jnp.broadcast_to(above, tile.shape), turn(tile, 1, 0)),
        )

    for k in range(modes + 1):
        coef_halo[0, k] = coef[0, k, rows - 1 : rows, :]
        coef_halo[1, k] = coef[0, k, 0:1, :]

    start_coef, finish_coef = exchange(
        coef_halo, "space", here, space, row_send_sem.at[fields], row_recv_sem.at[fields]
    )
    start_coef()

    def store_coef(k, face, tile, other):
        if k < modes:
            conduct[k, face] = 0.5 * (tile + other)
        else:
            drift[face] = 0.5 * (other - tile)

    for k in range(modes + 1):
        tile = coef[0, k]
        others = side_neighbours(
            tile, turn(coef[2, k], 1 - width), turn(coef[1, k], width - 1)
        )
        for face, other in enumerate(others):
            store_coef(k, 2 + face, tile, other)
        if k < modes:
            conduct[k, FACES] = tile

    finish_coef()
    for k in range(modes + 1):
        tile = coef[0, k]
        for face, other in enumerate(row_neighbours(tile, coef_halo[2, k], coef_halo[3, k])):
            store_coef(k, face, tile, other)

    def home(f, source, target):
        return pltpu.make_async_remote_copy(
            src_ref=result.at[f, target],
            dst_ref=back.at[f, source],
            send_sem=back_send_sem.at[f, target],
            recv_sem=back_recv_sem.at[f, source],
            device_id={"chaos": target},
            device_id_type=MESH,
        )

    def gather_field(f):
        @pl.loop(0, group)
        def _(step):
            source = peer_of(me, step, group)

            @pl.when(step < group - 1)
            def _():
                forth(f, source, source).wait_recv()

            for t in range(terms):
                tile = recv[f, source, t]
                row_halo[f, 0, source * terms + t] = tile[rows - 1 : rows]
                row_halo[f, 1, source * terms + t] = tile[0:1]

        start_rows, finish_rows = exchange(
            row_halo.at[f], "space", here, space, row_send_sem.at[f], row_recv_sem.at[f]
        )
        start_rows()
        return finish_rows

    def store_flux(f, j, face, tile, other):
        if f == 0:
            flux[0, j, face] = tile - other
        elif f == 1:
            flux[1, j, face] = (tile - other) - drift[face] * (tile + other) + flux[0, j, face]
        else:
            flux[2, j, face] = (tile - other) + drift[face] * (tile + other) - flux[0, j, face]

    def side_flux(f):
        @pl.loop(0, group)
        def _(source):
            rim = recv[0, source, terms]
            for t in range(terms):
                n = f * terms + t
                j = source * terms + t
                tile = recv[f, source, t]
                others = side_neighbours(
                    tile, turn(rim, -half - n), turn(rim, width - 1 - n)
                )
                for face, other in enumerate(others):
                    store_flux(f, j, 2 + face, tile, other)
                if f == 2:
                    centre[j] = recv[1, source, t] - tile

    def row_flux(f):
        @pl.loop(0, group)
        def _(source):
            for t in range(terms):
                j = source * terms + t
                tile = recv[f, source, t]
                others = row_neighbours(tile, row_halo[f, 2, j], row_halo[f, 3, j])
                for face, other in enumerate(others):
                    store_flux(f, j, face, tile, other)

    def apply(which):
        def send_home(step):
            for f in which:
                home(f, me, peer_of(me, step, group)).start()

        @pl.loop(0, group)
        def _(step):
            target = peer_of(me, step, group)
            for t in range(terms):
                total = {f: jnp.zeros((rows, lanes), jnp.float32) for f in which}
                for e in range(per_term):
                    entry = (target * terms + t) * per_term + e
                    j, k, value = table[1, entry], table[2, entry], values[entry]
                    if 0 in which:
                        total[0] += (value * conduct[k, FACES]) * centre[j]
                    for face in range(FACES):
                        h = value * conduct[k, face]
                        for f in which:
                            total[f] += h * flux[f, j, face]
                for f in which:
                    result[f, target, t] = total[f]

            @pl.when(step > 0)
            def _():
                send_home(step - 1)

        for f in which:
            for t in range(terms):
                back[f, me, t] = result[f, me, t]

    def place_field(f):
        @pl.loop(0, group - 1)
        def _(step):
            other = peer_of(me, step, group)
            home(f, other, other).wait_recv()

        @pl.loop(0, terms)
        def _(t):
            for q in range(chunks):
                part = [back[f, blocks * q + m, t] for m in range(blocks)]
                for p, tile in enumerate(swap_blocks(part)):
                    out[t * fields + f, p, :, lanes * q : lanes * (q + 1)] = tile

    finish_rows = gather_field(0)
    side_flux(0)
    finish_rows()
    row_flux(0)
    finish_rows = gather_field(1)
    side_flux(1)
    finish_rows()
    row_flux(1)
    apply((1,))
    finish_rows = gather_field(2)
    side_flux(2)
    finish_rows()
    row_flux(2)
    apply((0, 2))
    for f in (1, 0, 2):
        place_field(f)

    @pl.loop(0, group - 1)
    def _(step):
        target = peer_of(me, step, group)
        for f in range(fields):
            forth(f, me, target).wait_send()
            home(f, me, target).wait_send()


def solution(mesh):
    group, space = mesh.shape["chaos"], mesh.shape["space"]

    def shards(kl_fields, labels, region_scale, background, galerkin_table, triple_values, direction):
        terms, fields, planes, rows, columns = direction.shape
        modes, regions = kl_fields.shape[0], region_scale.shape[0]
        width = columns // group
        lanes = planes * width
        count = terms * fields
        all_terms = terms * group
        per_term = galerkin_table.shape[0] // all_terms
        dims = (group, space, terms, fields, planes, width, modes, regions, per_term)
        table = galerkin_table.T
        hbm = pl.BlockSpec(memory_space=pltpu.HBM)
        f32 = jnp.float32
        tile = (rows, lanes)
        dma = pltpu.SemaphoreType.DMA
        out = pl.pallas_call(
            functools.partial(kernel, dims),
            out_shape=jax.ShapeDtypeStruct((count, planes, rows, columns), f32),
            in_specs=[hbm] * 7,
            out_specs=pl.BlockSpec(memory_space=pltpu.VMEM),
            scratch_shapes=[
                pltpu.VMEM(kl_fields.shape, f32),
                pltpu.VMEM(labels.shape, jnp.int32),
                pltpu.VMEM(background.shape, f32),
                pltpu.VMEM((count, planes, rows, columns), f32),
                pltpu.SMEM(region_scale.shape, f32),
                pltpu.SMEM(table.shape, jnp.int32),
                pltpu.SMEM(triple_values.shape, f32),
                pltpu.VMEM((fields, group, terms + 1) + tile, f32),
                pltpu.VMEM((fields, group, terms + 1) + tile, f32),
                pltpu.VMEM((fields, group, terms) + tile, f32),
                pltpu.VMEM((fields, group, terms) + tile, f32),
                pltpu.VMEM((group, modes + 1) + tile, f32),
                pltpu.VMEM((group,) + tile, jnp.int32),
                pltpu.VMEM((3, modes + 1) + tile, f32),
                pltpu.VMEM((4, modes + 1, 1, lanes), f32),
                pltpu.VMEM((fields, 4, all_terms, 1, lanes), f32),
                pltpu.VMEM((modes, FACES + 1) + tile, f32),
                pltpu.VMEM((FACES,) + tile, f32),
                pltpu.VMEM((fields, all_terms, FACES) + tile, f32),
                pltpu.VMEM((all_terms,) + tile, f32),
                dma((7,)),
                dma((fields, group)),
                dma((fields, group)),
                dma((fields, group)),
                dma((fields, group)),
                dma((fields + 1, 2)),
                dma((fields + 1, 2)),
            ],
            compiler_params=pltpu.CompilerParams(
                collective_id=0, has_side_effects=True, vmem_limit_bytes=VMEM_BYTES
            ),
        )(
            *(
                pltpu.with_memory_space_constraint(x, pltpu.HBM)
                for x in (
                    kl_fields,
                    labels,
                    background,
                    direction.reshape(count, planes, rows, columns),
                    region_scale,
                    table,
                    triple_values,
                )
            )
        )
        return out.reshape(direction.shape)

    return jax.shard_map(
        shards,
        mesh=mesh,
        in_specs=(
            P(None, None, "space", None),
            P(None, "space", None),
            P(),
            P(None, "space", None),
            P(),
            P(),
            P("chaos", None, None, "space", None),
        ),
        out_specs=P("chaos", None, None, "space", None),
        check_vma=False,
    )
```
